256 devices in a mesh: seq: 64 (over y, z, core), head: 4 (over x).
Axes of the slice: x: 4, y: 4, z: 8, core: 2. Of those that a mesh axis runs over, the one named last changes fastest.
Arguments:
- queries: bfloat16 [12288, 4096], P('seq', 'head'), may hold values from -125 to 125
- key_vectors: bfloat16 [12288, 4096], P('seq', 'head'), may hold values from -21 to 21
- values: bfloat16 [12288, 4096], P('seq', 'head'), may hold values from -6 to 6
- cotangent: bfloat16 [12288, 4096], P('seq', 'head'), may hold values from -6 to 6
- cluster: int32 [12288, 1], P('seq'), may hold values from 0 to 15; in each aligned block of 192 rows (0 to 191, 192 to 383, ...) at most 24 rows name the same one
- block_pattern: int32 [16, 96, 96], replicated, may hold values from 0 to 1, as said below
Outputs:
- attended: bfloat16 [12288, 4096], P('seq', 'head')
- query_grad: bfloat16 [12288, 4096], P('seq', 'head')
- key_grad: bfloat16 [12288, 4096], P('seq', 'head')
- value_grad: bfloat16 [12288, 4096], P('seq', 'head')
The draws below stay inside these ranges and needn't reach their ends.
Inputs may be any that keep to these rules, and one draw needn't show every extreme that they name: Within the rows of one device no cluster is named by more than 24 rows, and in every draw some cluster is named by exactly 24 rows of some device. Every diagonal entry block_pattern[g, b, b] is 1.
All inputs are finite; a program needn't handle non-finite values.
Results may differ from the reference program's by a relative error of at most 0.0061.
Values may be sent and summed in bfloat16 or wider, within the bound.
A program may use at most 128 MiB of HBM per device.

```python
import math
import jax
import jax.numpy as jnp
import numpy as np
from jax import lax

HEADS = 32
HEAD_DIM = 128
T_DEV = 192
GS = 4
BLK = 128
SEQ = 12288
GROUPS = 16
CAP = 24
NB = 96


def draw_queries(key, part):
    first_key = jax.random.fold_in(key, 0)
    shape_full = (SEQ, HEADS * HEAD_DIM)
    return jnp.clip(jax.random.normal(first_key, shape_full, jnp.float32), -6.0, 6.0).astype(jnp.bfloat16)


def draw_key_vectors(key, part):
    first_key = jax.random.fold_in(key, 0)
    feature_total = HEADS * HEAD_DIM
    shape_full = (SEQ, feature_total)
    column_scale = 1.0 + 2.0 * jnp.arange(feature_total, dtype=jnp.float32) / feature_total
    return (jnp.clip(jax.random.normal(first_key, shape_full, jnp.float32), -6.0, 6.0) * column_scale[None, :]).astype(jnp.bfloat16)


def draw_block_pattern(key, part):
    random_bits = jax.random.randint(key, (GROUPS, NB, NB), 0, 2)
    diagonal_mask = jnp.arange(NB)[:, None] == jnp.arange(NB)[None, :]
    return jnp.where(diagonal_mask[None, :, :], 1, random_bits).astype(jnp.int32)


def block_scale(stream_key, extent, cuts, least, top_value):
    gain, own = 1.0, jax.random.fold_in(stream_key, 6)
    for position, parts in cuts:
        steps = jnp.exp(jax.random.uniform(jax.random.fold_in(own, position), (parts,), jnp.float32, least / len(cuts), top_value / len(cuts)))
        gain = gain * jnp.repeat(steps, extent[position] // parts).reshape([-1 if axis == position else 1 for axis in range(len(extent))])
    return gain


def assign_block(own_key, own, number, rows, number_of, top, most, skew):
    ranking = jax.random.permutation(own_key, number_of)
    heavy_load, ordinary = shares(number_of, rows * top, most, skew, True), shares(number_of, rows * top, most, skew, False)
    places = jnp.arange(number_of)

    def named(sizes, rotation):
        used = int((sizes > 0).sum())
        fixed = max(1, used // 4)
        passed = fixed + (places - fixed + rotation * (used - fixed)) % max(1, number_of - fixed)
        return jnp.zeros((number_of,), jnp.int32).at[ranking[jnp.where(places < fixed, places, passed)]].set(jnp.asarray(sizes, jnp.int32))

    sizes = jnp.where(number % 4 == 0, named(heavy_load, number // 4), named(ordinary, number - number // 4 - 1))
    mixed = jax.random.permutation(jax.random.fold_in(own, 3), number_of)
    giver, sink = mixed[0:number_of // 2 * 2:2], mixed[1:number_of // 2 * 2:2]
    margin = jnp.minimum(sizes[giver] - 1, most - sizes[sink]) // 2
    margin = jnp.where((giver == ranking[0]) | (sink == ranking[0]) | (sizes[sink] == 0), 0, jnp.maximum(margin, 0))
    passed = jax.random.randint(jax.random.fold_in(own, 4), (number_of // 2,), 0, 1 << 20) % (margin + 1)
    sizes = sizes.at[giver].add(-passed).at[sink].add(passed)
    labels = jnp.searchsorted(jnp.cumsum(sizes), jnp.arange(rows * top), side="right").astype(jnp.int32)
    grid = labels.reshape(top, rows).T
    grid = grid[jax.random.permutation(jax.random.fold_in(own, 1), rows)]
    rotation = jax.random.randint(jax.random.fold_in(own, 2), (rows, 1), 0, top)
    return jnp.take_along_axis(grid, (jnp.arange(top)[None, :] + rotation) % top, axis=1)


def shares(amount, total, limit, skew, full):
    portions = [(1 << 20) // math.isqrt(grade ** skew) + 1 for grade in range(1, amount + 1)]
    largest = limit if full else min(limit, max(-(-total // amount), total * portions[0] // sum(portions)))
    least = 1 if total - largest >= amount - 1 else 0
    given, surplus = [largest] + [least] * (amount - 1), total - largest - least * (amount - 1)
    while surplus > 0:
        movable = [i for i in range(1, amount) if given[i] < largest] or [i for i in range(1, amount) if given[i] < limit]
        whole, remaining = sum([portions[i] for i in movable]), surplus
        for i in movable:
            addition = min(limit - given[i], max(1, remaining * portions[i] // whole), surplus)
            given[i] = given[i] + addition
            surplus = surplus - addition
    return np.array(given)


def gaussian(stream_key, dims, spread, bound, cuts=(), kind=jnp.bfloat16):
    factor_of = block_scale(stream_key, dims, cuts, -0.22, 0.18) if cuts else 1.0
    drawn = jax.random.normal(stream_key, dims, jnp.float32) * spread * factor_of
    return jnp.minimum(jnp.maximum(drawn, -bound), bound).astype(kind)


def setup_inputs(seed: int = 0) -> dict:
    streams_of = jax.random.split(jax.random.key(seed), 7)
    queries = draw_queries(jax.random.fold_in(streams_of[6], 71), 0)
    key_vectors = draw_key_vectors(jax.random.fold_in(streams_of[6], 71), 0)
    values = gaussian(streams_of[2], (SEQ, HEADS * HEAD_DIM), 1.0, 6.0, ((0, 64), (1, 4)))
    cotangent = gaussian(streams_of[3], (SEQ, HEADS * HEAD_DIM), 1.0, 6.0, ((0, 64), (1, 4)))
    cluster_keys = jax.random.split(jax.random.fold_in(streams_of[4], 1), SEQ // T_DEV)
    cluster_turns = jax.random.permutation(jax.random.fold_in(streams_of[4], 3), SEQ // T_DEV)
    cluster = jax.vmap(lambda own, number: assign_block(jax.random.fold_in(streams_of[4], 2), own, number, T_DEV, GROUPS, 1, CAP, 2))(cluster_keys, cluster_turns).reshape((SEQ, 1))
    block_pattern = draw_block_pattern(jax.random.fold_in(streams_of[6], 71), 0)
    return {"queries": queries, "key_vectors": key_vectors, "values": values, "cotangent": cotangent, "cluster": cluster, "block_pattern": block_pattern}


NEG_FILL = -1e+30
EPSILON = 1e-05

def contract_last(left_side, right_side):
    return lax.dot_general(left_side, right_side, (((1,), (1,)), ((), ())), preferred_element_type=jnp.float32)

def contract_first(left_side, right_side):
    return lax.dot_general(left_side, right_side, (((0,), (0,)), ((), ())), preferred_element_type=jnp.float32)

def head_terms(query_rows, key_rows, value_rows, grad_rows, visible, score_scale):
    scores = jnp.where(visible, contract_last(query_rows, key_rows) * score_scale, NEG_FILL)
    row_max = lax.optimization_barrier(jnp.max(scores, axis=1, keepdims=True))
    weights = jnp.where(visible, jnp.exp(scores - row_max), 0.0)
    row_total = jnp.maximum(lax.optimization_barrier(jnp.sum(weights, axis=1, keepdims=True)), 1.0)
    probabilities = weights / row_total
    prob_half = probabilities.astype(jnp.bfloat16)
    attended = jnp.dot(prob_half, value_rows, preferred_element_type=jnp.float32).astype(jnp.bfloat16)
    prob_grad = contract_last(grad_rows, value_rows)
    row_delta = lax.optimization_barrier(jnp.sum(probabilities * prob_grad, axis=1, keepdims=True))
    score_grad = (probabilities * (prob_grad - row_delta)).astype(jnp.bfloat16)
    query_grad = (jnp.dot(score_grad, key_rows, preferred_element_type=jnp.float32) * score_scale).astype(jnp.bfloat16)
    key_grad = (contract_first(score_grad, query_rows) * score_scale).astype(jnp.bfloat16)
    value_grad = contract_first(prob_half, grad_rows).astype(jnp.bfloat16)
    return (attended, query_grad, key_grad, value_grad)

def reference(queries, key_vectors, values, cotangent, cluster, block_pattern):
    features = HEADS * HEAD_DIM
    score_scale = HEAD_DIM ** (-0.5)
    key_float = key_vectors.astype(jnp.float32)
    key_rms = jnp.sqrt(lax.optimization_barrier(jnp.mean(key_float * key_float, axis=1, keepdims=True)) + EPSILON)
    normed_float = key_float / key_rms
    normed = normed_float.astype(jnp.bfloat16)
    cluster_ids = cluster[:, 0].astype(jnp.int32)
    order = jnp.argsort(cluster_ids, stable=True).astype(jnp.int32)
    counts = lax.optimization_barrier(jnp.sum((cluster_ids[:, None] == jnp.arange(GROUPS, dtype=jnp.int32)[None, :]).astype(jnp.int32), axis=0))
    starts = (jnp.cumsum(counts) - counts).astype(jnp.int32)
    longest = GS * 2 * T_DEV
    padded = jnp.concatenate([order, jnp.full((longest,), SEQ, jnp.int32)])
    empty_half = jnp.zeros((SEQ, features), jnp.bfloat16)

    def per_cluster(running, cluster_index):
        taken = lax.dynamic_slice_in_dim(padded, starts[cluster_index], longest)
        present = jnp.arange(longest, dtype=jnp.int32) < counts[cluster_index]
        target = jnp.where(present, taken, SEQ).astype(jnp.int32)
        safe_rows = jnp.minimum(target, SEQ - 1)
        blocks = safe_rows // BLK
        pattern = lax.dynamic_index_in_dim(block_pattern, cluster_index, 0, keepdims=False)
        allowed = jnp.take(pattern[blocks], blocks, axis=1) == 1
        visible = allowed & (target[None, :] <= target[:, None]) & present[:, None] & present[None, :]
        query_rows = queries[safe_rows]
        key_rows = normed[safe_rows]
        value_rows = values[safe_rows]
        grad_rows = cotangent[safe_rows]

        def per_head(head_index):
            column_start = head_index * HEAD_DIM
            return head_terms(lax.dynamic_slice_in_dim(query_rows, column_start, HEAD_DIM, 1), lax.dynamic_slice_in_dim(key_rows, column_start, HEAD_DIM, 1), lax.dynamic_slice_in_dim(value_rows, column_start, HEAD_DIM, 1), lax.dynamic_slice_in_dim(grad_rows, column_start, HEAD_DIM, 1), visible, score_scale)
        results = lax.map(per_head, jnp.arange(HEADS, dtype=jnp.int32))
        updated = []
        for stored, result in zip(running, results):
            flat_result = jnp.transpose(result, (1, 0, 2)).reshape(longest, features)
            updated.append(stored.at[target].set(flat_result, mode='drop'))
        return (tuple(updated), None)
    finals, unused = lax.scan(per_cluster, (empty_half, empty_half, empty_half, empty_half), jnp.arange(GROUPS, dtype=jnp.int32))
    attended, query_grad, normed_grad, value_grad = finals
    grad_float = normed_grad.astype(jnp.float32)
    inner = lax.optimization_barrier(jnp.sum(normed_float * grad_float, axis=1, keepdims=True)) / features
    key_grad = ((grad_float - normed_float * inner) / key_rms).astype(jnp.bfloat16)
    return (attended, query_grad, key_grad, value_grad)
```

```python
import functools

import jax
import jax.numpy as jnp
import numpy as np
from jax import lax
from jax.experimental import pallas as pl
from jax.experimental.pallas import tpu as pltpu
from jax.sharding import PartitionSpec as P

HEADS = 32
HEAD_DIM = 128
BLK = 128
EPSILON = 1e-05
CAP = 24
NZ = 8
ND = 8
T_DEV = 192
GROUPS = 16
PAIR = 2 * CAP
ROWS = GROUPS * PAIR
SLOTS = 64 * CAP
QB = SLOTS // 4
CH = 128
BIG = 1e30
MESH = pl.DeviceIdType.MESH
F32 = jnp.float32
BF16 = jnp.bfloat16


def contract_last(left_side, right_side):
    return lax.dot_general(
        left_side, right_side, (((1,), (1,)), ((), ())), preferred_element_type=F32
    )


def place():
    me = lax.axis_index("seq")
    core = lax.rem(me, 2)
    z = lax.rem(me // 2, NZ)
    y = me // (2 * NZ)
    return y, z, core


def along_z(y, core, z):
    return (y * NZ + z) * 2 + core


def along_d(d, z):
    return ((d // 2) * NZ + z) * 2 + lax.rem(d, 2)


def greet(y, z, core, d):
    barrier = pltpu.get_barrier_semaphore()

    def signal(k, carry):
        pl.semaphore_signal(
            barrier,
            inc=1,
            device_id={"seq": along_z(y, core, lax.rem(z + k, NZ))},
            device_id_type=MESH,
        )
        pl.semaphore_signal(
            barrier,
            inc=1,
            device_id={"seq": along_d(lax.rem(d + k, ND), z)},
            device_id_type=MESH,
        )
        return carry

    lax.fori_loop(1, 8, signal, 0)
    pl.semaphore_wait(barrier, 14)


def head_columns(z):
    return pl.ds(pl.multiple_of(z * HEAD_DIM, HEAD_DIM), HEAD_DIM)


def pair_columns(d):
    return pl.ds(pl.multiple_of(d * 128, 128), 128)


def expander(slot_row, second):
    rows = lax.broadcasted_iota(jnp.int32, (ROWS, T_DEV), 0)
    hit = rows == slot_row[:, :T_DEV] + CAP * second
    return jnp.where(hit, 1.0, 0.0).astype(BF16)


def dispatch_kernel(
    slot_ref,
    meta_ref,
    v_ref,
    g_ref,
    q_ref,
    k_ref,
    out_ref,
    meta_out,
    slots_out,
    slots,
    metas,
    held,
    placing,
    sending,
    small_send,
    small_recv,
    meta_send,
    meta_recv,
    z_send,
    z_recv,
    d_send,
    d_recv,
    slots_sem,
):
    y, z, core = place()
    d = y * 2 + core
    sources = (v_ref, g_ref, q_ref, k_ref)
    greet(y, z, core, d)

    def small_copy(kind, k):
        to = lax.rem(z + k, NZ)
        if kind == 0:
            src, dst = slot_ref, slots.at[z]
        else:
            src, dst = meta_ref, metas.at[z]
        return pltpu.make_async_remote_copy(
            src_ref=src,
            dst_ref=dst,
            send_sem=small_send.at[kind, to],
            recv_sem=small_recv.at[kind, z],
            device_id={"seq": along_z(y, core, to)},
            device_id_type=MESH,
        )

    def small_arrival(kind, k):
        came = lax.rem(z + k, NZ)
        if kind == 0:
            src, dst = slot_ref, slots.at[came]
        else:
            src, dst = meta_ref, metas.at[came]
        return pltpu.make_async_remote_copy(
            src_ref=src,
            dst_ref=dst,
            send_sem=small_send.at[kind, came],
            recv_sem=small_recv.at[kind, came],
            device_id={"seq": along_z(y, core, came)},
            device_id_type=MESH,
        )

    def z_copy(a, k):
        to = lax.rem(z + k, NZ)
        return pltpu.make_async_remote_copy(
            src_ref=sources[a].at[:, head_columns(to)],
            dst_ref=held.at[a, z],
            send_sem=z_send.at[a, to],
            recv_sem=z_recv.at[a, z],
            device_id={"seq": along_z(y, core, to)},
            device_id_type=MESH,
        )

    def z_arrival(a, k):
        came = lax.rem(z + k, NZ)
        return pltpu.make_async_remote_copy(
            src_ref=held.at[a, came],
            dst_ref=held.at[a, came],
            send_sem=z_send.at[a, came],
            recv_sem=z_recv.at[a, came],
            device_id={"seq": along_z(y, core, came)},
            device_id_type=MESH,
        )

    def z_own(a):
        return pltpu.make_async_copy(
            sources[a].at[:, head_columns(z)], held.at[a, z], z_recv.at[a, z]
        )

    def d_copy(a, k):
        to = lax.rem(d + k, ND)
        return pltpu.make_async_remote_copy(
            src_ref=sending.at[a, :, to],
            dst_ref=out_ref.at[a, d],
            send_sem=d_send.at[a, to],
            recv_sem=d_recv.at[a, d],
            device_id={"seq": along_d(to, z)},
            device_id_type=MESH,
        )

    def d_arrival(a, k):
        came = lax.rem(d + k, ND)
        return pltpu.make_async_remote_copy(
            src_ref=out_ref.at[a, came],
            dst_ref=out_ref.at[a, came],
            send_sem=d_send.at[a, came],
            recv_sem=d_recv.at[a, came],
            device_id={"seq": along_d(came, z)},
            device_id_type=MESH,
        )

    def d_own(a):
        return pltpu.make_async_copy(sending.at[a, :, d], out_ref.at[a, d], d_recv.at[a, d])

    def meta_copy(k):
        to = lax.rem(d + k, ND)
        return pltpu.make_async_remote_copy(
            src_ref=metas.at[:, :, pair_columns(to)],
            dst_ref=meta_out.at[d],
            send_sem=meta_send.at[to],
            recv_sem=meta_recv.at[d],
            device_id={"seq": along_d(to, z)},
            device_id_type=MESH,
        )

    def meta_arrival(k):
        came = lax.rem(d + k, ND)
        return pltpu.make_async_remote_copy(
            src_ref=meta_out.at[came],
            dst_ref=meta_out.at[came],
            send_sem=meta_send.at[came],
            recv_sem=meta_recv.at[came],
            device_id={"seq": along_d(came, z)},
            device_id_type=MESH,
        )

    def meta_own():
        return pltpu.make_async_copy(
            metas.at[:, :, pair_columns(d)], meta_out.at[d], meta_recv.at[d]
        )

    def each(first, body):
        def step(k, carry):
            body(k)
            return carry

        lax.fori_loop(first, 8, step, 0)

    def start_small(k):
        small_copy(0, k).start()
        small_copy(1, k).start()

    each(1, start_small)
    own_slot = pltpu.make_async_copy(slot_ref, slots.at[z], small_recv.at[0, z])
    own_meta = pltpu.make_async_copy(meta_ref, metas.at[z], small_recv.at[1, z])
    own_slot.start()
    own_meta.start()
    for a in range(4):
        z_own(a).start()
        each(1, lambda k, a=a: z_copy(a, k).start())
    own_slot.wait()
    own_meta.wait()

    def finish_small(k):
        small_arrival(0, k).wait_recv()
        small_arrival(1, k).wait_recv()

    each(1, finish_small)
    keep_slots = pltpu.make_async_copy(slots, slots_out, slots_sem)
    keep_slots.start()
    meta_own().start()
    each(1, lambda k: meta_copy(k).start())

    def build(zz, carry):
        placing[zz] = expander(slots[zz], lax.rem(zz, 2))
        return carry

    lax.fori_loop(0, NZ, build, 0)

    def expand(a, carry):
        pltpu.make_async_copy(held.at[a, z], held.at[a, z], z_recv.at[a, z]).wait()
        each(1, lambda k: z_arrival(a, k).wait_recv())

        def pair(p, inner):
            rows = jnp.dot(placing[2 * p], held[a, 2 * p], preferred_element_type=F32)
            rows += jnp.dot(placing[2 * p + 1], held[a, 2 * p + 1], preferred_element_type=F32)
            sending[a, p] = rows.astype(BF16).reshape(ND, 2, PAIR, HEAD_DIM)
            return inner

        lax.fori_loop(0, NZ // 2, pair, 0)
        each(1, lambda k: d_copy(a, k).start())
        d_own(a).start()
        return carry

    lax.fori_loop(0, 4, expand, 0)

    def finish(a, carry):
        pltpu.make_async_copy(out_ref.at[a, d], out_ref.at[a, d], d_recv.at[a, d]).wait()

        def one(k):
            d_arrival(a, k).wait_recv()
            d_arrival(a, k).wait_send()
            z_arrival(a, k).wait_send()

        each(1, one)
        return carry

    lax.fori_loop(0, 4, finish, 0)
    keep_slots.wait()
    meta_own().wait()

    def finish_meta(k):
        small_arrival(0, k).wait_send()
        small_arrival(1, k).wait_send()
        meta_arrival(k).wait_recv()
        meta_arrival(k).wait_send()

    each(1, finish_meta)


def dispatch(slot_row, meta_row, v, g, q, k):
    any_space = pl.BlockSpec(memory_space=pl.ANY)
    dma = pltpu.SemaphoreType.DMA
    return pl.pallas_call(
        dispatch_kernel,
        out_shape=(
            jax.ShapeDtypeStruct((4, ND, NZ // 2, 2, PAIR, HEAD_DIM), BF16),
            jax.ShapeDtypeStruct((ND, NZ, 1, 128), F32),
            jax.ShapeDtypeStruct((NZ, 1, 256), jnp.int32),
        ),
        in_specs=[any_space] * 6,
        out_specs=(any_space,) * 3,
        scratch_shapes=[
            pltpu.VMEM((NZ, 1, 256), jnp.int32),
            pltpu.VMEM((NZ, 1, 1024), F32),
            pltpu.VMEM((4, NZ, T_DEV, HEAD_DIM), BF16),
            pltpu.VMEM((NZ, ROWS, T_DEV), BF16),
            pltpu.VMEM((4, NZ // 2, ND, 2, PAIR, HEAD_DIM), BF16),
            dma((2, NZ)),
            dma((2, NZ)),
            dma((ND,)),
            dma((ND,)),
            dma((4, NZ)),
            dma((4, NZ)),
            dma((4, ND)),
            dma((4, ND)),
            dma,
        ],
        compiler_params=pltpu.CompilerParams(collective_id=0, has_side_effects=True),
        name="dispatch",
    )(slot_row, meta_row, v, g, q, k)


def attention_kernel(
    score_scale,
    meta_ref,
    rep_ref,
    pick_ref,
    base_ref,
    pattern_ref,
    order_ref,
    v_ref,
    g_ref,
    q_ref,
    k_ref,
    o_ref,
    dq_ref,
    dk_ref,
    dv_ref,
    keys,
    queries,
    values,
    grads,
    key_t,
    value_t,
    scores,
    prob_grads,
    probs,
    score_grads,
    key_acc,
    value_acc,
):
    flat = (SLOTS, HEAD_DIM)
    numbers = jnp.dot(rep_ref[...], meta_ref[...].astype(BF16), preferred_element_type=F32)
    numbers = (numbers * pick_ref[...].astype(F32)).astype(BF16)
    number = jnp.dot(numbers, jnp.ones((128, 128), BF16), preferred_element_type=F32)
    lane = lax.broadcasted_iota(jnp.int32, flat, 1).astype(F32)
    position = base_ref[...].astype(F32) * 64.0 + number - 1.0
    low = lane * float(BLK)
    here = (number > 0.5) & (position >= low) & (position < low + float(BLK))
    dead = (number < 0.5) & (lane == 96.0)
    block = jnp.where(here | dead, 1.0, 0.0).astype(BF16)
    keys[:, :HEAD_DIM] = k_ref[...].reshape(flat)
    keys[:, HEAD_DIM:] = block
    queries[:, :HEAD_DIM] = q_ref[...].reshape(flat)
    hidden = jnp.dot(block, pattern_ref[...], preferred_element_type=F32)
    queries[:, HEAD_DIM:] = hidden.astype(BF16)
    values[...] = v_ref[...].reshape(flat)
    grads[...] = g_ref[...].reshape(flat)
    across = lax.broadcasted_iota(jnp.int32, (QB, QB), 1)
    eye = jnp.where(lax.broadcasted_iota(jnp.int32, (QB, QB), 0) == across, 1.0, 0.0).astype(BF16)
    small_eye = eye[:HEAD_DIM, :HEAD_DIM]
    key_t[...] = contract_last(small_eye, keys[:, :HEAD_DIM]).astype(BF16)
    value_t[...] = contract_last(small_eye, values[...]).astype(BF16)
    turn = score_scale * 1.4426950408889634

    def chunk(j, start=0):
        return pl.ds(pl.multiple_of(start + j * CH, CH), CH)

    def fold(piece, op):
        return op(piece.reshape(CH // 8, 8, QB), axis=0)

    for i in (3, 2, 1, 0):
        span = QB * (i + 1)
        query_rows = queries[QB * i : span, :]
        grad_rows = grads[QB * i : span, :]

        def full_scores(j, running):
            piece = contract_last(keys[chunk(j), :], query_rows)
            scores[chunk(j), :] = piece
            return jnp.maximum(running, fold(piece, jnp.max))

        def edge_scores(j, running):
            piece = contract_last(keys[chunk(j, QB * i), :], query_rows)
            piece += order_ref[chunk(j), :].astype(F32)
            scores[chunk(j, QB * i), :] = piece
            return jnp.maximum(running, fold(piece, jnp.max))

        top = jnp.full((8, QB), -3e38, F32)
        if i:
            top = lax.fori_loop(0, 3 * i, full_scores, top)
        top = lax.fori_loop(0, 3, edge_scores, top)
        top = jnp.max(top, axis=0, keepdims=True)

        def weigh(j, running):
            total, delta = running
            weights = jnp.exp2((scores[chunk(j), :] - top) * turn)
            scores[chunk(j), :] = weights
            terms = contract_last(values[chunk(j), :], grad_rows)
            prob_grads[chunk(j), :] = terms
            return (total + fold(weights, jnp.sum), delta + fold(weights * terms, jnp.sum))

        zero = jnp.zeros((8, QB), F32)
        total, delta = lax.fori_loop(0, 3 * (i + 1), weigh, (zero, zero))
        inverse = 1.0 / jnp.maximum(jnp.sum(total, axis=0, keepdims=True), 1.0)
        delta = jnp.sum(delta, axis=0, keepdims=True) * inverse

        def settle(j, carry):
            shares = scores[chunk(j), :] * inverse
            half = shares.astype(BF16)
            probs[chunk(j), :] = half
            slopes = (shares * (prob_grads[chunk(j), :] - delta)).astype(BF16)
            score_grads[chunk(j), :] = slopes
            value_part = jnp.dot(half, grad_rows, preferred_element_type=F32)
            key_part = jnp.dot(slopes, query_rows[:, :HEAD_DIM], preferred_element_type=F32)
            if i == 3:
                value_acc[chunk(j), :] = value_part
                key_acc[chunk(j), :] = key_part
            else:
                value_acc[chunk(j), :] += value_part
                key_acc[chunk(j), :] += key_part
            return carry

        lax.fori_loop(0, 3 * (i + 1), settle, 0)
        shape = (2, NZ // 2, PAIR, HEAD_DIM)
        attended_t = jnp.dot(value_t[:, :span], probs[:span, :], preferred_element_type=F32)
        attended = contract_last(eye, attended_t.astype(BF16))
        o_ref[2 * i : 2 * i + 2] = attended.astype(BF16).reshape(shape)
        query_t = jnp.dot(key_t[:, :span], score_grads[:span, :], preferred_element_type=F32)
        query_grad = contract_last(eye, (query_t * score_scale).astype(BF16))
        dq_ref[2 * i : 2 * i + 2] = query_grad.astype(BF16).reshape(shape)

    whole = (ND, NZ // 2, PAIR, HEAD_DIM)
    dk_ref[...] = (key_acc[...] * score_scale).astype(BF16).reshape(whole)
    dv_ref[...] = value_acc[...].astype(BF16).reshape(whole)


def slot_tables():
    order = np.arange(SLOTS)
    rank = order % CAP
    z = order // CAP % NZ
    d = order // (CAP * NZ)
    source = (d // 2) * 16 + z * 2 + d % 2
    arrival = d * NZ + z
    rep = (arrival[:, None] == np.arange(64)[None, :]).astype(np.float32)
    lanes = np.arange(128)[None, :]
    pick = np.stack([(lanes == (rank + CAP * unit)[:, None]) for unit in range(2)])
    base = np.broadcast_to((source * 3)[:, None], (SLOTS, 128)).astype(np.float32)
    sequence = (source * CAP + rank)[:QB]
    hidden = np.where(sequence[:, None] > sequence[None, :], -BIG, 0.0).astype(np.float32)
    return rep, pick.astype(np.float32), base, hidden


def attention(meta, pattern, arrived):
    rep, pick, base, hidden = slot_tables()
    fixed = lambda *zeros: lambda unit: zeros
    piece = (None, ND, NZ // 2, None, PAIR, HEAD_DIM)
    in_specs = [
        pl.BlockSpec((64, 128), fixed(0, 0)),
        pl.BlockSpec((SLOTS, 64), fixed(0, 0)),
        pl.BlockSpec((None, SLOTS, 128), lambda unit: (unit, 0, 0)),
        pl.BlockSpec((SLOTS, 128), fixed(0, 0)),
        pl.BlockSpec((None, 128, 128), lambda unit: (unit, 0, 0)),
        pl.BlockSpec((QB, QB), fixed(0, 0)),
    ]
    for a in range(4):
        in_specs.append(pl.BlockSpec(piece, lambda unit, a=a: (a, 0, 0, unit, 0, 0)))
    out_shape = jax.ShapeDtypeStruct((ND, NZ // 2, 2, PAIR, HEAD_DIM), BF16)
    out_spec = pl.BlockSpec(piece[1:], lambda unit: (0, 0, unit, 0, 0))
    vmem = pltpu.VMEM
    return pl.pallas_call(
        functools.partial(attention_kernel, HEAD_DIM ** (-0.5)),
        out_shape=(out_shape,) * 4,
        grid=(2,),
        in_specs=in_specs,
        out_specs=(out_spec,) * 4,
        scratch_shapes=[
            vmem((SLOTS, 256), BF16),
            vmem((SLOTS, 256), BF16),
            vmem((SLOTS, HEAD_DIM), BF16),
            vmem((SLOTS, HEAD_DIM), BF16),
            vmem((HEAD_DIM, SLOTS), BF16),
            vmem((HEAD_DIM, SLOTS), BF16),
            vmem((SLOTS, QB), F32),
            vmem((SLOTS, QB), F32),
            vmem((SLOTS, QB), BF16),
            vmem((SLOTS, QB), BF16),
            vmem((SLOTS, HEAD_DIM), F32),
            vmem((SLOTS, HEAD_DIM), F32),
        ],
        name="attention",
    )(
        meta,
        jnp.asarray(rep, BF16),
        jnp.asarray(pick, BF16),
        jnp.asarray(base, BF16),
        pattern,
        jnp.asarray(hidden, BF16),
        arrived,
        arrived,
        arrived,
        arrived,
    )


def combine_kernel(
    slots_ref,
    dk_ref,
    o_ref,
    dq_ref,
    dv_ref,
    dk_home,
    o_home,
    dq_home,
    dv_home,
    held,
    placing,
    sending,
    d_send,
    d_recv,
    z_send,
    z_recv,
):
    y, z, core = place()
    d = y * 2 + core
    sources = (dk_ref, o_ref, dq_ref, dv_ref)
    homes = (dk_home, o_home, dq_home, dv_home)
    greet(y, z, core, d)

    def d_copy(a, k):
        to = lax.rem(d + k, ND)
        return pltpu.make_async_remote_copy(
            src_ref=sources[a].at[to],
            dst_ref=held.at[a, d],
            send_sem=d_send.at[a, to],
            recv_sem=d_recv.at[a, d],
            device_id={"seq": along_d(to, z)},
            device_id_type=MESH,
        )

    def d_arrival(a, k):
        came = lax.rem(d + k, ND)
        return pltpu.make_async_remote_copy(
            src_ref=held.at[a, came],
            dst_ref=held.at[a, came],
            send_sem=d_send.at[a, came],
            recv_sem=d_recv.at[a, came],
            device_id={"seq": along_d(came, z)},
            device_id_type=MESH,
        )

    def z_copy(a, k):
        to = lax.rem(z + k, NZ)
        return pltpu.make_async_remote_copy(
            src_ref=sending.at[a, to],
            dst_ref=homes[a].at[:, head_columns(z)],
            send_sem=z_send.at[a, to],
            recv_sem=z_recv.at[a, z],
            device_id={"seq": along_z(y, core, to)},
            device_id_type=MESH,
        )

    def z_arrival(a, k):
        came = lax.rem(z + k, NZ)
        return pltpu.make_async_remote_copy(
            src_ref=sending.at[a, came],
            dst_ref=homes[a].at[:, head_columns(came)],
            send_sem=z_send.at[a, came],
            recv_sem=z_recv.at[a, came],
            device_id={"seq": along_z(y, core, came)},
            device_id_type=MESH,
        )

    def z_own(a):
        return pltpu.make_async_copy(
            sending.at[a, z], homes[a].at[:, head_columns(z)], z_recv.at[a, z]
        )

    def each(first, body):
        def step(k, carry):
            body(k)
            return carry

        lax.fori_loop(first, 8, step, 0)

    for a in range(4):
        each(1, lambda k, a=a: d_copy(a, k).start())
        pltpu.make_async_copy(sources[a].at[d], held.at[a, d], d_recv.at[a, d]).start()

    across = lax.broadcasted_iota(jnp.int32, (T_DEV, T_DEV), 1)
    down = lax.broadcasted_iota(jnp.int32, (T_DEV, T_DEV), 0)
    eye = jnp.where(down == across, 1.0, 0.0).astype(BF16)

    def build(zz, carry):
        there = expander(slots_ref[zz], lax.rem(zz, 2))
        placing[zz] = contract_last(eye, there).astype(BF16)
        return carry

    lax.fori_loop(0, NZ, build, 0)

    for a in range(4):
        pltpu.make_async_copy(held.at[a, d], held.at[a, d], d_recv.at[a, d]).wait()
        each(1, lambda k, a=a: d_arrival(a, k).wait_recv())

        def gather(k, a=a):
            to = lax.rem(z + k, NZ)
            rows = held[a, :, to // 2].reshape(ROWS, HEAD_DIM)
            found = jnp.dot(placing[to], rows, preferred_element_type=F32)
            sending[a, to] = found.astype(BF16)

        def gather_send(k, a=a):
            gather(k)
            z_copy(a, k).start()

        each(1, gather_send)
        gather(0)
        z_own(a).start()

    for a in range(4):
        z_own(a).wait()

        def one(k, a=a):
            z_arrival(a, k).wait_recv()
            z_arrival(a, k).wait_send()
            d_arrival(a, k).wait_send()

        each(1, one)


def combine(slots, dk, o, dq, dv):
    any_space = pl.BlockSpec(memory_space=pl.ANY)
    dma = pltpu.SemaphoreType.DMA
    home = jax.ShapeDtypeStruct((T_DEV, NZ * HEAD_DIM), BF16)
    return pl.pallas_call(
        combine_kernel,
        out_shape=(home,) * 4,
        in_specs=[pl.BlockSpec(memory_space=pltpu.VMEM)] + [any_space] * 4,
        out_specs=(any_space,) * 4,
        scratch_shapes=[
            pltpu.VMEM((4, ND, NZ // 2, 2, PAIR, HEAD_DIM), BF16),
            pltpu.VMEM((NZ, T_DEV, ROWS), BF16),
            pltpu.VMEM((4, NZ, T_DEV, HEAD_DIM), BF16),
            dma((4, ND)),
            dma((4, ND)),
            dma((4, NZ)),
            dma((4, NZ)),
        ],
        compiler_params=pltpu.CompilerParams(collective_id=1, has_side_effects=True),
        name="combine",
    )(slots, dk, o, dq, dv)


def per_device(queries, key_vectors, values, cotangent, cluster, block_pattern):
    me = lax.axis_index("seq")
    d = (me // (2 * NZ)) * 2 + me % 2
    key_float = key_vectors.astype(F32)
    square_sum = lax.psum(jnp.sum(key_float * key_float, axis=1), "head")
    key_rms = jnp.sqrt(square_sum / (HEADS * HEAD_DIM) + EPSILON)[:, None]
    normed_float = key_float / key_rms
    normed = normed_float.astype(BF16)
    ids = cluster[:, 0]
    token = jnp.arange(T_DEV, dtype=jnp.int32)
    earlier = (ids[:, None] == ids[None, :]) & (token[:, None] < token[None, :])
    rank = jnp.sum(earlier.astype(jnp.int32), axis=0)
    slot = ids * PAIR + rank
    slot_row = jnp.pad(slot, (0, 256 - T_DEV), constant_values=-1).reshape(1, 256)
    meta_slot = (ids // 2) * 128 + (ids % 2) * CAP + rank
    spots = jnp.arange(ND * 128, dtype=jnp.int32)
    hit = meta_slot[:, None] == spots[None, :]
    meta_row = jnp.sum(jnp.where(hit, (token + 1).astype(F32)[:, None], 0.0), axis=0)
    arrived, meta, slots = dispatch(
        slot_row, meta_row.reshape(1, ND * 128), values, cotangent, queries, normed
    )
    pattern = lax.dynamic_slice_in_dim(block_pattern, 2 * d, 2, 0)
    blocks = pattern.shape[1]
    pattern = jnp.where(pattern == 1, 0.0, -BIG)
    pattern = jnp.pad(pattern, ((0, 0), (0, 0), (0, 1)), constant_values=-BIG)
    pattern = jnp.pad(pattern, ((0, 0), (0, 128 - blocks), (0, 127 - blocks))).astype(BF16)
    o, dq, dk, dv = attention(meta.reshape(64, 128), pattern, arrived)
    grad_rows, attended, query_grad, value_grad = combine(slots, dk, o, dq, dv)
    grad_float = grad_rows.astype(F32)
    inner = lax.psum(jnp.sum(normed_float * grad_float, axis=1), "head")
    key_grad = (
        (grad_float - normed_float * (inner / (HEADS * HEAD_DIM))[:, None]) / key_rms
    ).astype(BF16)
    return (attended, query_grad, key_grad, value_grad)


def solution(mesh):
    in_specs = (
        P("seq", "head"),
        P("seq", "head"),
        P("seq", "head"),
        P("seq", "head"),
        P("seq", None),
        P(),
    )
    out_specs = (P("seq", "head"), P("seq", "head"), P("seq", "head"), P("seq", "head"))
    return jax.shard_map(
        per_device, mesh=mesh, in_specs=in_specs, out_specs=out_specs, check_vma=False
    )
```

```python
import functools

import jax
import jax.numpy as jnp
import numpy as np
from jax import lax
from jax.experimental import pallas as pl
from jax.experimental.pallas import tpu as pltpu
from jax.sharding import PartitionSpec as P

HEADS = 32
HEAD_DIM = 128
BLK = 128
EPSILON = 1e-05
CAP = 24
NZ = 8
ND = 8
T_DEV = 192
GROUPS = 16
PAIR = 2 * CAP
ROWS = GROUPS * PAIR
SLOTS = 64 * CAP
QB = SLOTS // 4
BIG = 1e30
MESH = pl.DeviceIdType.MESH
F32 = jnp.float32
BF16 = jnp.bfloat16


def contract_last(left_side, right_side):
    return lax.dot_general(
        left_side, right_side, (((1,), (1,)), ((), ())), preferred_element_type=F32
    )


def place():
    me = lax.axis_index("seq")
    core = lax.rem(me, 2)
    z = lax.rem(me // 2, NZ)
    y = me // (2 * NZ)
    return y, z, core


def along_z(y, core, z):
    return (y * NZ + z) * 2 + core


def along_d(d, z):
    return ((d // 2) * NZ + z) * 2 + lax.rem(d, 2)


def greet(y, z, core, d):
    barrier = pltpu.get_barrier_semaphore()

    def signal(k, carry):
        pl.semaphore_signal(
            barrier,
            inc=1,
            device_id={"seq": along_z(y, core, lax.rem(z + k, NZ))},
            device_id_type=MESH,
        )
        pl.semaphore_signal(
            barrier,
            inc=1,
            device_id={"seq": along_d(lax.rem(d + k, ND), z)},
            device_id_type=MESH,
        )
        return carry

    lax.fori_loop(1, 8, signal, 0)
    pl.semaphore_wait(barrier, 14)


def head_columns(z):
    return pl.ds(pl.multiple_of(z * HEAD_DIM, HEAD_DIM), HEAD_DIM)


def pair_columns(d):
    return pl.ds(pl.multiple_of(d * 128, 128), 128)


def expander(slot_row, second):
    rows = lax.broadcasted_iota(jnp.int32, (ROWS, T_DEV), 0)
    hit = rows == slot_row[:, :T_DEV] + CAP * second
    return jnp.where(hit, 1.0, 0.0).astype(BF16)


def dispatch_kernel(
    slot_ref,
    meta_ref,
    v_ref,
    g_ref,
    q_ref,
    k_ref,
    out_ref,
    meta_out,
    slots_out,
    slots,
    metas,
    held,
    placing,
    sending,
    landed,
    out_sem,
    small_send,
    small_recv,
    meta_send,
    meta_recv,
    z_send,
    z_recv,
    d_send,
    d_recv,
    slots_sem,
):
    y, z, core = place()
    d = y * 2 + core
    sources = (v_ref, g_ref, q_ref, k_ref)
    greet(y, z, core, d)

    def small_copy(kind, k):
        to = lax.rem(z + k, NZ)
        if kind == 0:
            src, dst = slot_ref, slots.at[z]
        else:
            src, dst = meta_ref, metas.at[z]
        return pltpu.make_async_remote_copy(
            src_ref=src,
            dst_ref=dst,
            send_sem=small_send.at[kind, to],
            recv_sem=small_recv.at[kind, z],
            device_id={"seq": along_z(y, core, to)},
            device_id_type=MESH,
        )

    def small_arrival(kind, k):
        came = lax.rem(z + k, NZ)
        if kind == 0:
            src, dst = slot_ref, slots.at[came]
        else:
            src, dst = meta_ref, metas.at[came]
        return pltpu.make_async_remote_copy(
            src_ref=src,
            dst_ref=dst,
            send_sem=small_send.at[kind, came],
            recv_sem=small_recv.at[kind, came],
            device_id={"seq": along_z(y, core, came)},
            device_id_type=MESH,
        )

    def z_copy(a, k):
        to = lax.rem(z + k, NZ)
        return pltpu.make_async_remote_copy(
            src_ref=sources[a].at[:, head_columns(to)],
            dst_ref=held.at[a, z],
            send_sem=z_send.at[a, to],
            recv_sem=z_recv.at[a, z],
            device_id={"seq": along_z(y, core, to)},
            device_id_type=MESH,
        )

    def z_arrival(a, k):
        came = lax.rem(z + k, NZ)
        return pltpu.make_async_remote_copy(
            src_ref=held.at[a, came],
            dst_ref=held.at[a, came],
            send_sem=z_send.at[a, came],
            recv_sem=z_recv.at[a, came],
            device_id={"seq": along_z(y, core, came)},
            device_id_type=MESH,
        )

    def z_own(a):
        return pltpu.make_async_copy(
            sources[a].at[:, head_columns(z)], held.at[a, z], z_recv.at[a, z]
        )

    def d_copy(a, k):
        to = lax.rem(d + k, ND)
        return pltpu.make_async_remote_copy(
            src_ref=sending.at[a, :, to],
            dst_ref=landed.at[a, d],
            send_sem=d_send.at[a, to],
            recv_sem=d_recv.at[a, d],
            device_id={"seq": along_d(to, z)},
            device_id_type=MESH,
        )

    def d_arrival(a, k):
        came = lax.rem(d + k, ND)
        return pltpu.make_async_remote_copy(
            src_ref=landed.at[a, came],
            dst_ref=landed.at[a, came],
            send_sem=d_send.at[a, came],
            recv_sem=d_recv.at[a, came],
            device_id={"seq": along_d(came, z)},
            device_id_type=MESH,
        )

    def d_own(a):
        return pltpu.make_async_copy(sending.at[a, :, d], landed.at[a, d], d_recv.at[a, d])

    def put_out(a):
        return pltpu.make_async_copy(landed.at[a], out_ref.at[a], out_sem.at[a])

    def meta_copy(k):
        to = lax.rem(d + k, ND)
        return pltpu.make_async_remote_copy(
            src_ref=metas.at[:, :, pair_columns(to)],
            dst_ref=meta_out.at[d],
            send_sem=meta_send.at[to],
            recv_sem=meta_recv.at[d],
            device_id={"seq": along_d(to, z)},
            device_id_type=MESH,
        )

    def meta_arrival(k):
        came = lax.rem(d + k, ND)
        return pltpu.make_async_remote_copy(
            src_ref=meta_out.at[came],
            dst_ref=meta_out.at[came],
            send_sem=meta_send.at[came],
            recv_sem=meta_recv.at[came],
            device_id={"seq": along_d(came, z)},
            device_id_type=MESH,
        )

    def meta_own():
        return pltpu.make_async_copy(
            metas.at[:, :, pair_columns(d)], meta_out.at[d], meta_recv.at[d]
        )

    def each(first, body):
        def step(k, carry):
            body(k)
            return carry

        lax.fori_loop(first, 8, step, 0)

    def start_small(k):
        small_copy(0, k).start()
        small_copy(1, k).start()

    each(1, start_small)
    own_slot = pltpu.make_async_copy(slot_ref, slots.at[z], small_recv.at[0, z])
    own_meta = pltpu.make_async_copy(meta_ref, metas.at[z], small_recv.at[1, z])
    own_slot.start()
    own_meta.start()
    for a in range(4):
        z_own(a).start()
        each(1, lambda k, a=a: z_copy(a, k).start())
    own_slot.wait()
    own_meta.wait()

    def finish_small(k):
        small_arrival(0, k).wait_recv()
        small_arrival(1, k).wait_recv()

    each(1, finish_small)
    keep_slots = pltpu.make_async_copy(slots, slots_out, slots_sem)
    keep_slots.start()
    meta_own().start()
    each(1, lambda k: meta_copy(k).start())

    def build(zz, carry):
        placing[zz] = expander(slots[zz], lax.rem(zz, 2))
        return carry

    lax.fori_loop(0, NZ, build, 0)

    def expand(a, carry):
        pltpu.make_async_copy(held.at[a, z], held.at[a, z], z_recv.at[a, z]).wait()
        each(1, lambda k: z_arrival(a, k).wait_recv())

        def pair(p, inner):
            rows = jnp.dot(placing[2 * p], held[a, 2 * p], preferred_element_type=F32)
            rows += jnp.dot(placing[2 * p + 1], held[a, 2 * p + 1], preferred_element_type=F32)
            sending[a, p] = rows.astype(BF16).reshape(ND, 2, PAIR, HEAD_DIM)
            return inner

        lax.fori_loop(0, NZ // 2, pair, 0)
        each(1, lambda k: d_copy(a, k).start())
        d_own(a).start()
        return carry

    lax.fori_loop(0, 4, expand, 0)

    def finish(a, carry):
        d_own(a).wait()
        each(1, lambda k: d_arrival(a, k).wait_recv())
        put_out(a).start()

        def one(k):
            d_arrival(a, k).wait_send()
            z_arrival(a, k).wait_send()

        each(1, one)
        return carry

    lax.fori_loop(0, 4, finish, 0)

    def close(a, carry):
        put_out(a).wait()
        return carry

    lax.fori_loop(0, 4, close, 0)
    keep_slots.wait()
    meta_own().wait()

    def finish_meta(k):
        small_arrival(0, k).wait_send()
        small_arrival(1, k).wait_send()
        meta_arrival(k).wait_recv()
        meta_arrival(k).wait_send()

    each(1, finish_meta)


def dispatch(slot_row, meta_row, v, g, q, k):
    any_space = pl.BlockSpec(memory_space=pl.ANY)
    dma = pltpu.SemaphoreType.DMA
    return pl.pallas_call(
        dispatch_kernel,
        out_shape=(
            jax.ShapeDtypeStruct((4, ND, NZ // 2, 2, PAIR, HEAD_DIM), BF16),
            jax.ShapeDtypeStruct((ND, NZ, 1, 128), F32),
            jax.ShapeDtypeStruct((NZ, 1, 256), jnp.int32),
        ),
        in_specs=[any_space] * 6,
        out_specs=(any_space,) * 3,
        scratch_shapes=[
            pltpu.VMEM((NZ, 1, 256), jnp.int32),
            pltpu.VMEM((NZ, 1, 1024), F32),
            pltpu.VMEM((4, NZ, T_DEV, HEAD_DIM), BF16),
            pltpu.VMEM((NZ, ROWS, T_DEV), BF16),
            pltpu.VMEM((4, NZ // 2, ND, 2, PAIR, HEAD_DIM), BF16),
            pltpu.VMEM((4, ND, NZ // 2, 2, PAIR, HEAD_DIM), BF16),
            dma((4,)),
            dma((2, NZ)),
            dma((2, NZ)),
            dma((ND,)),
            dma((ND,)),
            dma((4, NZ)),
            dma((4, NZ)),
            dma((4, ND)),
            dma((4, ND)),
            dma,
        ],
        compiler_params=pltpu.CompilerParams(collective_id=0, has_side_effects=True),
        name="dispatch",
    )(slot_row, meta_row, v, g, q, k)


def attention_kernel(
    score_scale,
    meta_ref,
    rep_ref,
    pick_ref,
    base_ref,
    pattern_ref,
    order_ref,
    v_ref,
    g_ref,
    q_ref,
    k_ref,
    o_ref,
    dq_ref,
    dk_ref,
    dv_ref,
    keys,
    queries,
    values,
    grads,
    key_t,
    value_t,
    scores,
    prob_grads,
    probs,
    score_grads,
):
    flat = (SLOTS, HEAD_DIM)
    numbers = jnp.dot(rep_ref[...], meta_ref[...].astype(BF16), preferred_element_type=F32)
    numbers = (numbers * pick_ref[...].astype(F32)).astype(BF16)
    number = jnp.dot(numbers, jnp.ones((128, 128), BF16), preferred_element_type=F32)
    lane = lax.broadcasted_iota(jnp.int32, flat, 1).astype(F32)
    position = base_ref[...].astype(F32) * 64.0 + number - 1.0
    low = lane * float(BLK)
    here = (number > 0.5) & (position >= low) & (position < low + float(BLK))
    dead = (number < 0.5) & (lane == 96.0)
    block = jnp.where(here | dead, 1.0, 0.0).astype(BF16)
    keys[:, :HEAD_DIM] = k_ref[...].reshape(flat)
    keys[:, HEAD_DIM:] = block
    queries[:, :HEAD_DIM] = q_ref[...].reshape(flat)
    hidden = jnp.dot(block, pattern_ref[...], preferred_element_type=F32)
    queries[:, HEAD_DIM:] = hidden.astype(BF16)
    values[...] = v_ref[...].reshape(flat)
    grads[...] = g_ref[...].reshape(flat)
    across = lax.broadcasted_iota(jnp.int32, (QB, QB), 1)
    eye = jnp.where(lax.broadcasted_iota(jnp.int32, (QB, QB), 0) == across, 1.0, 0.0).astype(BF16)
    small_eye = eye[:HEAD_DIM, :HEAD_DIM]
    key_t[...] = contract_last(small_eye, keys[:, :HEAD_DIM]).astype(BF16)
    value_t[...] = contract_last(small_eye, values[...]).astype(BF16)
    turn = score_scale * 1.4426950408889634

    shape = (2, NZ // 2, PAIR, HEAD_DIM)

    def fold(piece, op):
        return op(piece.reshape(QB // 8, 8, QB), axis=0)

    def part(j):
        return pl.ds(QB * j, QB)

    for i in range(4):
        span = QB * (i + 1)
        query_rows = queries[part(i), :]
        grad_rows = grads[part(i), :]
        side = i % 2
        top = None
        for j in range(i + 1):
            piece = contract_last(keys[part(j), :], query_rows)
            if j == i:
                piece += order_ref[...].astype(F32)
            scores[side, part(j), :] = piece
            most = fold(piece, jnp.max)
            top = most if top is None else jnp.maximum(top, most)
        top = jnp.max(top, axis=0, keepdims=True)
        total = jnp.zeros((8, QB), F32)
        delta = jnp.zeros((8, QB), F32)
        for j in range(i + 1):
            terms = contract_last(values[part(j), :], grad_rows)
            prob_grads[side, part(j), :] = terms
            weights = jnp.exp2((scores[side, part(j), :] - top) * turn)
            scores[side, part(j), :] = weights
            total += fold(weights, jnp.sum)
            delta += fold(weights * terms, jnp.sum)
        inverse = 1.0 / jnp.maximum(jnp.sum(total, axis=0, keepdims=True), 1.0)
        delta = jnp.sum(delta, axis=0, keepdims=True) * inverse
        for j in range(i + 1):
            shares = scores[side, part(j), :] * inverse
            probs[part(j), part(i)] = shares.astype(BF16)
            slopes = shares * (prob_grads[side, part(j), :] - delta)
            score_grads[part(j), part(i)] = slopes.astype(BF16)
        attended_t = jnp.dot(value_t[:, :span], probs[:span, part(i)], preferred_element_type=F32)
        attended = contract_last(eye, attended_t.astype(BF16))
        o_ref[2 * i : 2 * i + 2] = attended.astype(BF16).reshape(shape)
        query_t = jnp.dot(key_t[:, :span], score_grads[:span, part(i)], preferred_element_type=F32)
        query_grad = contract_last(eye, (query_t * score_scale).astype(BF16))
        dq_ref[2 * i : 2 * i + 2] = query_grad.astype(BF16).reshape(shape)

    for j in range(4):
        first = QB * j
        slopes = score_grads[part(j), first:]
        key_grad = jnp.dot(slopes, queries[first:, :HEAD_DIM], preferred_element_type=F32)
        dk_ref[2 * j : 2 * j + 2] = (key_grad * score_scale).astype(BF16).reshape(shape)
        value_grad = jnp.dot(probs[part(j), first:], grads[first:, :], preferred_element_type=F32)
        dv_ref[2 * j : 2 * j + 2] = value_grad.astype(BF16).reshape(shape)


def slot_tables():
    order = np.arange(SLOTS)
    rank = order % CAP
    z = order // CAP % NZ
    d = order // (CAP * NZ)
    source = (d // 2) * 16 + z * 2 + d % 2
    arrival = d * NZ + z
    rep = (arrival[:, None] == np.arange(64)[None, :]).astype(np.float32)
    lanes = np.arange(128)[None, :]
    pick = np.stack([(lanes == (rank + CAP * unit)[:, None]) for unit in range(2)])
    base = np.broadcast_to((source * 3)[:, None], (SLOTS, 128)).astype(np.float32)
    sequence = (source * CAP + rank)[:QB]
    hidden = np.where(sequence[:, None] > sequence[None, :], -BIG, 0.0).astype(np.float32)
    return rep, pick.astype(np.float32), base, hidden


def attention(meta, pattern, arrived):
    rep, pick, base, hidden = slot_tables()
    fixed = lambda *zeros: lambda unit: zeros
    piece = (None, ND, NZ // 2, None, PAIR, HEAD_DIM)
    in_specs = [
        pl.BlockSpec((64, 128), fixed(0, 0)),
        pl.BlockSpec((SLOTS, 64), fixed(0, 0)),
        pl.BlockSpec((None, SLOTS, 128), lambda unit: (unit, 0, 0)),
        pl.BlockSpec((SLOTS, 128), fixed(0, 0)),
        pl.BlockSpec((None, 128, 128), lambda unit: (unit, 0, 0)),
        pl.BlockSpec((QB, QB), fixed(0, 0)),
    ]
    for a in range(4):
        in_specs.append(pl.BlockSpec(piece, lambda unit, a=a: (a, 0, 0, unit, 0, 0)))
    out_shape = jax.ShapeDtypeStruct((ND, NZ // 2, 2, PAIR, HEAD_DIM), BF16)
    out_spec = pl.BlockSpec(piece[1:], lambda unit: (0, 0, unit, 0, 0))
    vmem = pltpu.VMEM
    return pl.pallas_call(
        functools.partial(attention_kernel, HEAD_DIM ** (-0.5)),
        out_shape=(out_shape,) * 4,
        grid=(2,),
        in_specs=in_specs,
        out_specs=(out_spec,) * 4,
        scratch_shapes=[
            vmem((SLOTS, 256), BF16),
            vmem((SLOTS, 256), BF16),
            vmem((SLOTS, HEAD_DIM), BF16),
            vmem((SLOTS, HEAD_DIM), BF16),
            vmem((HEAD_DIM, SLOTS), BF16),
            vmem((HEAD_DIM, SLOTS), BF16),
            vmem((2, SLOTS, QB), F32),
            vmem((2, SLOTS, QB), F32),
            vmem((SLOTS, SLOTS), BF16),
            vmem((SLOTS, SLOTS), BF16),
        ],
        name="attention",
    )(
        meta,
        jnp.asarray(rep, BF16),
        jnp.asarray(pick, BF16),
        jnp.asarray(base, BF16),
        pattern,
        jnp.asarray(hidden, BF16),
        arrived,
        arrived,
        arrived,
        arrived,
    )


def combine_kernel(
    slots_ref,
    dk_ref,
    o_ref,
    dq_ref,
    dv_ref,
    dk_home,
    o_home,
    dq_home,
    dv_home,
    held,
    placing,
    sending,
    landed,
    out_sem,
    d_send,
    d_recv,
    z_send,
    z_recv,
):
    y, z, core = place()
    d = y * 2 + core
    sources = (dk_ref, o_ref, dq_ref, dv_ref)
    homes = (dk_home, o_home, dq_home, dv_home)
    greet(y, z, core, d)

    def d_copy(a, k):
        to = lax.rem(d + k, ND)
        return pltpu.make_async_remote_copy(
            src_ref=sources[a].at[to],
            dst_ref=held.at[a, d],
            send_sem=d_send.at[a, to],
            recv_sem=d_recv.at[a, d],
            device_id={"seq": along_d(to, z)},
            device_id_type=MESH,
        )

    def d_arrival(a, k):
        came = lax.rem(d + k, ND)
        return pltpu.make_async_remote_copy(
            src_ref=held.at[a, came],
            dst_ref=held.at[a, came],
            send_sem=d_send.at[a, came],
            recv_sem=d_recv.at[a, came],
            device_id={"seq": along_d(came, z)},
            device_id_type=MESH,
        )

    def z_copy(a, k):
        to = lax.rem(z + k, NZ)
        return pltpu.make_async_remote_copy(
            src_ref=sending.at[a, to],
            dst_ref=landed.at[a, :, head_columns(z)],
            send_sem=z_send.at[a, to],
            recv_sem=z_recv.at[a, z],
            device_id={"seq": along_z(y, core, to)},
            device_id_type=MESH,
        )

    def z_arrival(a, k):
        came = lax.rem(z + k, NZ)
        return pltpu.make_async_remote_copy(
            src_ref=sending.at[a, came],
            dst_ref=landed.at[a, :, head_columns(came)],
            send_sem=z_send.at[a, came],
            recv_sem=z_recv.at[a, came],
            device_id={"seq": along_z(y, core, came)},
            device_id_type=MESH,
        )

    def z_own(a):
        return pltpu.make_async_copy(
            sending.at[a, z], landed.at[a, :, head_columns(z)], z_recv.at[a, z]
        )

    def each(first, body):
        def step(k, carry):
            body(k)
            return carry

        lax.fori_loop(first, 8, step, 0)

    for a in range(4):
        each(1, lambda k, a=a: d_copy(a, k).start())
        pltpu.make_async_copy(sources[a].at[d], held.at[a, d], d_recv.at[a, d]).start()

    across = lax.broadcasted_iota(jnp.int32, (T_DEV, T_DEV), 1)
    down = lax.broadcasted_iota(jnp.int32, (T_DEV, T_DEV), 0)
    eye = jnp.where(down == across, 1.0, 0.0).astype(BF16)

    def build(zz, carry):
        there = expander(slots_ref[zz], lax.rem(zz, 2))
        placing[zz] = contract_last(eye, there).astype(BF16)
        return carry

    lax.fori_loop(0, NZ, build, 0)

    for a in range(4):
        pltpu.make_async_copy(held.at[a, d], held.at[a, d], d_recv.at[a, d]).wait()
        each(1, lambda k, a=a: d_arrival(a, k).wait_recv())

        def gather(k, a=a):
            to = lax.rem(z + k, NZ)
            rows = held[a, :, to // 2].reshape(ROWS, HEAD_DIM)
            found = jnp.dot(placing[to], rows, preferred_element_type=F32)
            sending[a, to] = found.astype(BF16)

        def gather_send(k, a=a):
            gather(k)
            z_copy(a, k).start()

        each(1, gather_send)
        gather(0)
        z_own(a).start()

    def put_out(a):
        return pltpu.make_async_copy(landed.at[a], homes[a], out_sem.at[a])

    for a in range(4):
        z_own(a).wait()
        each(1, lambda k, a=a: z_arrival(a, k).wait_recv())
        put_out(a).start()

    for a in range(4):

        def one(k, a=a):
            z_arrival(a, k).wait_send()
            d_arrival(a, k).wait_send()

        each(1, one)
        put_out(a).wait()


def combine(slots, dk, o, dq, dv):
    any_space = pl.BlockSpec(memory_space=pl.ANY)
    dma = pltpu.SemaphoreType.DMA
    home = jax.ShapeDtypeStruct((T_DEV, NZ * HEAD_DIM), BF16)
    return pl.pallas_call(
        combine_kernel,
        out_shape=(home,) * 4,
        in_specs=[pl.BlockSpec(memory_space=pltpu.VMEM)] + [any_space] * 4,
        out_specs=(any_space,) * 4,
        scratch_shapes=[
            pltpu.VMEM((4, ND, NZ // 2, 2, PAIR, HEAD_DIM), BF16),
            pltpu.VMEM((NZ, T_DEV, ROWS), BF16),
            pltpu.VMEM((4, NZ, T_DEV, HEAD_DIM), BF16),
            pltpu.VMEM((4, T_DEV, NZ * HEAD_DIM), BF16),
            dma((4,)),
            dma((4, ND)),
            dma((4, ND)),
            dma((4, NZ)),
            dma((4, NZ)),
        ],
        compiler_params=pltpu.CompilerParams(collective_id=1, has_side_effects=True),
        name="combine",
    )(slots, dk, o, dq, dv)


def per_device(queries, key_vectors, values, cotangent, cluster, block_pattern):
    me = lax.axis_index("seq")
    d = (me // (2 * NZ)) * 2 + me % 2
    key_float = key_vectors.astype(F32)
    square_sum = lax.psum(jnp.sum(key_float * key_float, axis=1), "head")
    key_rms = jnp.sqrt(square_sum / (HEADS * HEAD_DIM) + EPSILON)[:, None]
    normed_float = key_float / key_rms
    normed = normed_float.astype(BF16)
    ids = cluster[:, 0]
    token = jnp.arange(T_DEV, dtype=jnp.int32)
    earlier = (ids[:, None] == ids[None, :]) & (token[:, None] < token[None, :])
    rank = jnp.sum(earlier.astype(jnp.int32), axis=0)
    slot = ids * PAIR + rank
    slot_row = jnp.pad(slot, (0, 256 - T_DEV), constant_values=-1).reshape(1, 256)
    meta_slot = (ids // 2) * 128 + (ids % 2) * CAP + rank
    spots = jnp.arange(ND * 128, dtype=jnp.int32)
    hit = meta_slot[:, None] == spots[None, :]
    meta_row = jnp.sum(jnp.where(hit, (token + 1).astype(F32)[:, None], 0.0), axis=0)
    arrived, meta, slots = dispatch(
        slot_row, meta_row.reshape(1, ND * 128), values, cotangent, queries, normed
    )
    pattern = lax.dynamic_slice_in_dim(block_pattern, 2 * d, 2, 0)
    blocks = pattern.shape[1]
    pattern = jnp.where(pattern == 1, 0.0, -BIG)
    pattern = jnp.pad(pattern, ((0, 0), (0, 0), (0, 1)), constant_values=-BIG)
    pattern = jnp.pad(pattern, ((0, 0), (0, 128 - blocks), (0, 127 - blocks))).astype(BF16)
    o, dq, dk, dv = attention(meta.reshape(64, 128), pattern, arrived)
    grad_rows, attended, query_grad, value_grad = combine(slots, dk, o, dq, dv)
    grad_float = grad_rows.astype(F32)
    inner = lax.psum(jnp.sum(normed_float * grad_float, axis=1), "head")
    key_grad = (
        (grad_float - normed_float * (inner / (HEADS * HEAD_DIM))[:, None]) / key_rms
    ).astype(BF16)
    return (attended, query_grad, key_grad, value_grad)


def solution(mesh):
    in_specs = (
        P("seq", "head"),
        P("seq", "head"),
        P("seq", "head"),
        P("seq", "head"),
        P("seq", None),
        P(),
    )
    out_specs = (P("seq", "head"), P("seq", "head"), P("seq", "head"), P("seq", "head"))
    return jax.shard_map(
        per_device, mesh=mesh, in_specs=in_specs, out_specs=out_specs, check_vma=False
    )
```

```python
import functools

import jax
import jax.numpy as jnp
import numpy as np
from jax import lax
from jax.experimental import pallas as pl
from jax.experimental.pallas import tpu as pltpu
from jax.sharding import PartitionSpec as P

HEADS = 32
HEAD_DIM = 128
BLK = 128
EPSILON = 1e-05
CAP = 24
NZ = 8
ND = 8
NX = 4
T_DEV = 192
GROUPS = 16
PAIR = 2 * CAP
ROWS = GROUPS * PAIR
SLOTS = 64 * CAP
QB = SLOTS // 4
BIG = 1e30
MESH = pl.DeviceIdType.MESH
F32 = jnp.float32
BF16 = jnp.bfloat16


def contract_last(left_side, right_side):
    return lax.dot_general(
        left_side, right_side, (((1,), (1,)), ((), ())), preferred_element_type=F32
    )


def place():
    me = lax.axis_index("seq")
    core = lax.rem(me, 2)
    z = lax.rem(me // 2, NZ)
    y = me // (2 * NZ)
    return y, z, core


def along_z(y, core, z):
    return (y * NZ + z) * 2 + core


def along_d(d, z):
    return ((d // 2) * NZ + z) * 2 + lax.rem(d, 2)


def greet(y, z, core, d, x):
    barrier = pltpu.get_barrier_semaphore()

    def signal(k, carry):
        pl.semaphore_signal(
            barrier,
            inc=1,
            device_id={"seq": along_z(y, core, lax.rem(z + k, NZ))},
            device_id_type=MESH,
        )
        pl.semaphore_signal(
            barrier,
            inc=1,
            device_id={"seq": along_d(lax.rem(d + k, ND), z)},
            device_id_type=MESH,
        )
        return carry

    lax.fori_loop(1, 8, signal, 0)

    def signal_x(k, carry):
        pl.semaphore_signal(
            barrier, inc=1, device_id={"head": lax.rem(x + k, NX)}, device_id_type=MESH
        )
        return carry

    lax.fori_loop(1, NX, signal_x, 0)
    return barrier


def head_columns(z):
    return pl.ds(pl.multiple_of(z * HEAD_DIM, HEAD_DIM), HEAD_DIM)


def pair_columns(d):
    return pl.ds(pl.multiple_of(d * 128, 128), 128)


def expander(slot_row, second):
    rows = lax.broadcasted_iota(jnp.int32, (ROWS, T_DEV), 0)
    hit = rows == slot_row[:, :T_DEV] + CAP * second
    return jnp.where(hit, 1.0, 0.0).astype(BF16)


def each(first, body, last=8):
    def step(k, carry):
        body(k)
        return carry

    lax.fori_loop(first, last, step, 0)


def x_copies(x, parts, send, recv):
    def copy(k):
        to = lax.rem(x + k, NX)
        return pltpu.make_async_remote_copy(
            src_ref=parts.at[x],
            dst_ref=parts.at[x],
            send_sem=send.at[to],
            recv_sem=recv.at[x],
            device_id={"head": to},
            device_id_type=MESH,
        )

    def arrival(k):
        came = lax.rem(x + k, NX)
        return pltpu.make_async_remote_copy(
            src_ref=parts.at[came],
            dst_ref=parts.at[came],
            send_sem=send.at[came],
            recv_sem=recv.at[came],
            device_id={"head": came},
            device_id_type=MESH,
        )

    return copy, arrival


def lanes_summed(wide):
    return sum(wide[:, HEAD_DIM * j : HEAD_DIM * (j + 1)] for j in range(NZ))


def dispatch_kernel(
    ids_ref,
    key_ref,
    v_ref,
    g_ref,
    q_ref,
    out_ref,
    meta_out,
    slots_out,
    rms_out,
    own_slot,
    own_meta,
    slots,
    metas,
    parts,
    normed,
    held,
    placing,
    sending,
    landed,
    out_sem,
    small_send,
    small_recv,
    meta_send,
    meta_recv,
    x_send,
    x_recv,
    z_send,
    z_recv,
    d_send,
    d_recv,
    slots_sem,
):
    y, z, core = place()
    d = y * 2 + core
    x = lax.axis_index("head")
    q0 = lax.rem(z, 4)
    sources = (v_ref, g_ref, q_ref, normed)
    barrier = greet(y, z, core, d, x)

    key_float = key_ref[...].astype(F32)
    parts[x] = lanes_summed(key_float * key_float)
    ids = ids_ref[...]
    down = lax.broadcasted_iota(jnp.int32, (T_DEV, T_DEV), 0)
    across = lax.broadcasted_iota(jnp.int32, (T_DEV, T_DEV), 1)
    ids_float = ids.astype(F32)
    spread = jnp.where(down == across, ids_float, 0.0).astype(BF16)
    column = jnp.dot(spread, jnp.ones((T_DEV, T_DEV), BF16), preferred_element_type=F32)
    earlier = (column == ids_float) & (down < across)
    rank = jnp.sum(jnp.where(earlier, 1.0, 0.0), axis=0, keepdims=True).astype(jnp.int32)
    own_slot[...] = jnp.full((1, 256), -1, jnp.int32)
    own_slot[:, :T_DEV] = ids * PAIR + rank
    meta_slot = (ids // 2) * 128 + (ids - (ids // 2) * 2) * CAP + rank
    spots = lax.broadcasted_iota(jnp.int32, (ND * 128, T_DEV), 0)
    spotted = jnp.where(spots == meta_slot, 1.0, 0.0).astype(BF16)
    numbers = (lax.broadcasted_iota(jnp.int32, (8, T_DEV), 1) + 1).astype(F32).astype(BF16)
    own_meta[...] = contract_last(numbers, spotted)[0:1, :]

    def small_copy(kind, k):
        to = lax.rem(z + k, NZ)
        src, dst = (own_slot, slots) if kind == 0 else (own_meta, metas)
        return pltpu.make_async_remote_copy(
            src_ref=src,
            dst_ref=dst.at[z],
            send_sem=small_send.at[kind, to],
            recv_sem=small_recv.at[kind, z],
            device_id={"seq": along_z(y, core, to)},
            device_id_type=MESH,
        )

    def small_arrival(kind, k):
        came = lax.rem(z + k, NZ)
        src, dst = (own_slot, slots) if kind == 0 else (own_meta, metas)
        return pltpu.make_async_remote_copy(
            src_ref=src,
            dst_ref=dst.at[came],
            send_sem=small_send.at[kind, came],
            recv_sem=small_recv.at[kind, came],
            device_id={"seq": along_z(y, core, came)},
            device_id_type=MESH,
        )

    def z_copy(a, to):
        return pltpu.make_async_remote_copy(
            src_ref=sources[a].at[:, head_columns(to)],
            dst_ref=held.at[a, q0, z // 4],
            send_sem=z_send.at[a, to],
            recv_sem=z_recv.at[a, q0],
            device_id={"seq": along_z(y, core, to)},
            device_id_type=MESH,
        )

    def z_sent(a, k):
        to = lax.rem(z + k, NZ)
        return pltpu.make_async_remote_copy(
            src_ref=held.at[a, q0, z // 4],
            dst_ref=held.at[a, q0, z // 4],
            send_sem=z_send.at[a, to],
            recv_sem=z_recv.at[a, q0],
            device_id={"seq": along_z(y, core, to)},
            device_id_type=MESH,
        )

    def z_start(a):
        pltpu.make_async_copy(
            sources[a].at[:, head_columns(z)], held.at[a, q0, z // 4], z_recv.at[a, q0]
        ).start()
        z_copy(a, lax.rem(z + 4, NZ)).start()

        def both(o):
            z_copy(a, lax.rem(z + NZ - o, NZ)).start()
            z_copy(a, lax.rem(z + 4 - o, NZ)).start()

        each(1, both, 4)

    def d_copy(a, q, k):
        to = lax.rem(d + k, ND)
        return pltpu.make_async_remote_copy(
            src_ref=sending.at[a, q, to],
            dst_ref=landed.at[a, d, q],
            send_sem=d_send.at[a, to],
            recv_sem=d_recv.at[a, d],
            device_id={"seq": along_d(to, z)},
            device_id_type=MESH,
        )

    def d_arrival(a, k):
        came = lax.rem(d + k, ND)
        return pltpu.make_async_remote_copy(
            src_ref=landed.at[a, came],
            dst_ref=landed.at[a, came],
            send_sem=d_send.at[a, came],
            recv_sem=d_recv.at[a, came],
            device_id={"seq": along_d(came, z)},
            device_id_type=MESH,
        )

    def put_out(a):
        return pltpu.make_async_copy(landed.at[a], out_ref.at[a], out_sem.at[a])

    def meta_copy(k):
        to = lax.rem(d + k, ND)
        return pltpu.make_async_remote_copy(
            src_ref=metas.at[:, :, pair_columns(to)],
            dst_ref=meta_out.at[d],
            send_sem=meta_send.at[to],
            recv_sem=meta_recv.at[d],
            device_id={"seq": along_d(to, z)},
            device_id_type=MESH,
        )

    def meta_arrival(k):
        came = lax.rem(d + k, ND)
        return pltpu.make_async_remote_copy(
            src_ref=meta_out.at[came],
            dst_ref=meta_out.at[came],
            send_sem=meta_send.at[came],
            recv_sem=meta_recv.at[came],
            device_id={"seq": along_d(came, z)},
            device_id_type=MESH,
        )

    def meta_own():
        return pltpu.make_async_copy(
            metas.at[:, :, pair_columns(d)], meta_out.at[d], meta_recv.at[d]
        )

    x_copy, x_arrival = x_copies(x, parts, x_send, x_recv)
    pl.semaphore_wait(barrier, 17)
    each(1, lambda k: x_copy(k).start(), NX)

    def start_small(k):
        small_copy(0, k).start()
        small_copy(1, k).start()

    each(1, start_small)
    own_slot_copy = pltpu.make_async_copy(own_slot, slots.at[z], small_recv.at[0, z])
    own_meta_copy = pltpu.make_async_copy(own_meta, metas.at[z], small_recv.at[1, z])
    own_slot_copy.start()
    own_meta_copy.start()
    for a in range(3):
        z_start(a)
    each(1, lambda k: x_arrival(k).wait_recv(), NX)
    square = parts[0] + parts[1] + parts[2] + parts[3]
    square = jnp.sum(square, axis=1, keepdims=True)
    key_rms = jnp.sqrt(square / (HEADS * HEAD_DIM) + EPSILON)
    rms_out[...] = jnp.broadcast_to(key_rms, (T_DEV, HEAD_DIM))
    normed[...] = (key_ref[...].astype(F32) / key_rms).astype(BF16)
    own_slot_copy.wait()
    own_meta_copy.wait()
    z_start(3)

    def finish_small(k):
        small_arrival(0, k).wait_recv()
        small_arrival(1, k).wait_recv()

    each(1, finish_small)
    keep_slots = pltpu.make_async_copy(slots, slots_out, slots_sem)
    keep_slots.start()
    meta_own().start()
    each(1, lambda k: meta_copy(k).start())
    each(0, lambda q: placing.__setitem__((q, 0), expander(slots[q], 0)), 4)
    each(0, lambda q: placing.__setitem__((q, 1), expander(slots[q + 4], 1)), 4)

    def expand(a, carry):
        def pair(o):
            q = lax.rem(z + o, 4)
            pltpu.make_async_copy(held.at[a, q], held.at[a, q], z_recv.at[a, q]).wait()
            rows = jnp.dot(placing[q, 0], held[a, q, 0], preferred_element_type=F32)
            rows += jnp.dot(placing[q, 1], held[a, q, 1], preferred_element_type=F32)
            sending[a, q] = rows.astype(BF16).reshape(ND, 2, PAIR, HEAD_DIM)
            each(1, lambda k: d_copy(a, q, k).start())
            pltpu.make_async_copy(
                sending.at[a, q, d], landed.at[a, d, q], d_recv.at[a, d]
            ).start()

        each(0, pair, 4)
        return carry

    lax.fori_loop(0, 4, expand, 0)

    def finish(a, carry):
        pltpu.make_async_copy(landed.at[a, d], landed.at[a, d], d_recv.at[a, d]).wait()
        each(1, lambda k: d_arrival(a, k).wait_recv())
        put_out(a).start()

        def one(k):
            d_arrival(a, k).wait_send()
            z_sent(a, k).wait_send()

        each(1, one)
        return carry

    lax.fori_loop(0, 4, finish, 0)
    each(0, lambda a: put_out(a).wait(), 4)
    each(1, lambda k: x_arrival(k).wait_send(), NX)
    keep_slots.wait()
    meta_own().wait()

    def finish_meta(k):
        small_arrival(0, k).wait_send()
        small_arrival(1, k).wait_send()
        meta_arrival(k).wait_recv()
        meta_arrival(k).wait_send()

    each(1, finish_meta)


def dispatch(ids, key, v, g, q):
    any_space = pl.BlockSpec(memory_space=pl.ANY)
    near = pl.BlockSpec(memory_space=pltpu.VMEM)
    dma = pltpu.SemaphoreType.DMA
    vmem = pltpu.VMEM
    return pl.pallas_call(
        dispatch_kernel,
        out_shape=(
            jax.ShapeDtypeStruct((4, ND, NZ // 2, 2, PAIR, HEAD_DIM), BF16),
            jax.ShapeDtypeStruct((ND, NZ, 1, 128), F32),
            jax.ShapeDtypeStruct((NZ, 1, 256), jnp.int32),
            jax.ShapeDtypeStruct((T_DEV, HEAD_DIM), F32),
        ),
        in_specs=[near, near] + [any_space] * 3,
        out_specs=(any_space,) * 3 + (near,),
        scratch_shapes=[
            vmem((1, 256), jnp.int32),
            vmem((1, ND * 128), F32),
            vmem((NZ, 1, 256), jnp.int32),
            vmem((NZ, 1, ND * 128), F32),
            vmem((NX, T_DEV, HEAD_DIM), F32),
            vmem((T_DEV, NZ * HEAD_DIM), BF16),
            vmem((4, NZ // 2, 2, T_DEV, HEAD_DIM), BF16),
            vmem((NZ // 2, 2, ROWS, T_DEV), BF16),
            vmem((4, NZ // 2, ND, 2, PAIR, HEAD_DIM), BF16),
            vmem((4, ND, NZ // 2, 2, PAIR, HEAD_DIM), BF16),
            dma((4,)),
            dma((2, NZ)),
            dma((2, NZ)),
            dma((ND,)),
            dma((ND,)),
            dma((NX,)),
            dma((NX,)),
            dma((4, NZ)),
            dma((4, NZ // 2)),
            dma((4, ND)),
            dma((4, ND)),
            dma,
        ],
        compiler_params=pltpu.CompilerParams(collective_id=0, has_side_effects=True),
        name="dispatch",
    )(ids, key, v, g, q)


def attention_kernel(
    score_scale,
    meta_ref,
    rep_ref,
    pick_ref,
    base_ref,
    pattern_ref,
    order_ref,
    v_ref,
    g_ref,
    q_ref,
    k_ref,
    o_ref,
    dq_ref,
    dk_ref,
    dv_ref,
    keys,
    queries,
    values,
    grads,
    key_t,
    value_t,
    scores,
    prob_grads,
    probs,
    score_grads,
):
    flat = (SLOTS, HEAD_DIM)
    numbers = jnp.dot(rep_ref[...], meta_ref[...].astype(BF16), preferred_element_type=F32)
    numbers = (numbers * pick_ref[...].astype(F32)).astype(BF16)
    number = jnp.dot(numbers, jnp.ones((128, 128), BF16), preferred_element_type=F32)
    lane = lax.broadcasted_iota(jnp.int32, flat, 1).astype(F32)
    position = base_ref[...].astype(F32) * 64.0 + number - 1.0
    low = lane * float(BLK)
    here = (number > 0.5) & (position >= low) & (position < low + float(BLK))
    dead = (number < 0.5) & (lane == 96.0)
    block = jnp.where(here | dead, 1.0, 0.0).astype(BF16)
    keys[:, :HEAD_DIM] = k_ref[...].reshape(flat)
    keys[:, HEAD_DIM:] = block
    queries[:, :HEAD_DIM] = q_ref[...].reshape(flat)
    hidden = jnp.dot(block, pattern_ref[...], preferred_element_type=F32)
    queries[:, HEAD_DIM:] = hidden.astype(BF16)
    values[...] = v_ref[...].reshape(flat)
    grads[...] = g_ref[...].reshape(flat)
    across = lax.broadcasted_iota(jnp.int32, (QB, QB), 1)
    eye = jnp.where(lax.broadcasted_iota(jnp.int32, (QB, QB), 0) == across, 1.0, 0.0).astype(BF16)
    small_eye = eye[:HEAD_DIM, :HEAD_DIM]
    key_t[...] = contract_last(small_eye, keys[:, :HEAD_DIM]).astype(BF16)
    value_t[...] = contract_last(small_eye, values[...]).astype(BF16)
    turn = score_scale * 1.4426950408889634

    shape = (2, NZ // 2, PAIR, HEAD_DIM)

    def fold(piece, op):
        return op(piece.reshape(QB // 8, 8, QB), axis=0)

    def part(j):
        return pl.ds(QB * j, QB)

    for i in range(4):
        span = QB * (i + 1)
        query_rows = queries[part(i), :]
        grad_rows = grads[part(i), :]
        side = i % 2
        top = None
        for j in range(i + 1):
            piece = contract_last(keys[part(j), :], query_rows)
            if j == i:
                piece += order_ref[...].astype(F32)
            scores[side, part(j), :] = piece
            most = fold(piece, jnp.max)
            top = most if top is None else jnp.maximum(top, most)
        top = jnp.max(top, axis=0, keepdims=True)
        total = jnp.zeros((8, QB), F32)
        delta = jnp.zeros((8, QB), F32)
        for j in range(i + 1):
            terms = contract_last(values[part(j), :], grad_rows)
            prob_grads[side, part(j), :] = terms
            weights = jnp.exp2((scores[side, part(j), :] - top) * turn)
            scores[side, part(j), :] = weights
            total += fold(weights, jnp.sum)
            delta += fold(weights * terms, jnp.sum)
        inverse = 1.0 / jnp.maximum(jnp.sum(total, axis=0, keepdims=True), 1.0)
        delta = jnp.sum(delta, axis=0, keepdims=True) * inverse
        for j in range(i + 1):
            shares = scores[side, part(j), :] * inverse
            probs[part(j), part(i)] = shares.astype(BF16)
            slopes = shares * (prob_grads[side, part(j), :] - delta)
            score_grads[part(j), part(i)] = slopes.astype(BF16)
        attended_t = jnp.dot(value_t[:, :span], probs[:span, part(i)], preferred_element_type=F32)
        attended = contract_last(eye, attended_t.astype(BF16))
        o_ref[2 * i : 2 * i + 2] = attended.astype(BF16).reshape(shape)
        query_t = jnp.dot(key_t[:, :span], score_grads[:span, part(i)], preferred_element_type=F32)
        query_grad = contract_last(eye, (query_t * score_scale).astype(BF16))
        dq_ref[2 * i : 2 * i + 2] = query_grad.astype(BF16).reshape(shape)

    for j in range(4):
        first = QB * j
        slopes = score_grads[part(j), first:]
        key_grad = jnp.dot(slopes, queries[first:, :HEAD_DIM], preferred_element_type=F32)
        dk_ref[2 * j : 2 * j + 2] = (key_grad * score_scale).astype(BF16).reshape(shape)
        value_grad = jnp.dot(probs[part(j), first:], grads[first:, :], preferred_element_type=F32)
        dv_ref[2 * j : 2 * j + 2] = value_grad.astype(BF16).reshape(shape)


def slot_tables():
    order = np.arange(SLOTS)
    rank = order % CAP
    pair = order // CAP % NZ
    z = pair // 2 + 4 * (pair % 2)
    d = order // (CAP * NZ)
    source = (d // 2) * 16 + z * 2 + d % 2
    arrival = d * NZ + z
    rep = (arrival[:, None] == np.arange(64)[None, :]).astype(np.float32)
    lanes = np.arange(128)[None, :]
    pick = np.stack([(lanes == (rank + CAP * unit)[:, None]) for unit in range(2)])
    base = np.broadcast_to((source * 3)[:, None], (SLOTS, 128)).astype(np.float32)
    sequence = (source * CAP + rank)[:QB]
    hidden = np.where(sequence[:, None] > sequence[None, :], -BIG, 0.0).astype(np.float32)
    return rep, pick.astype(np.float32), base, hidden


def attention(meta, pattern, arrived):
    rep, pick, base, hidden = slot_tables()
    fixed = lambda *zeros: lambda unit: zeros
    piece = (None, ND, NZ // 2, None, PAIR, HEAD_DIM)
    in_specs = [
        pl.BlockSpec((64, 128), fixed(0, 0)),
        pl.BlockSpec((SLOTS, 64), fixed(0, 0)),
        pl.BlockSpec((None, SLOTS, 128), lambda unit: (unit, 0, 0)),
        pl.BlockSpec((SLOTS, 128), fixed(0, 0)),
        pl.BlockSpec((None, 128, 128), lambda unit: (unit, 0, 0)),
        pl.BlockSpec((QB, QB), fixed(0, 0)),
    ]
    for a in range(4):
        in_specs.append(pl.BlockSpec(piece, lambda unit, a=a: (a, 0, 0, unit, 0, 0)))
    out_shape = jax.ShapeDtypeStruct((ND, NZ // 2, 2, PAIR, HEAD_DIM), BF16)
    out_spec = pl.BlockSpec(piece[1:], lambda unit: (0, 0, unit, 0, 0))
    vmem = pltpu.VMEM
    return pl.pallas_call(
        functools.partial(attention_kernel, HEAD_DIM ** (-0.5)),
        out_shape=(out_shape,) * 4,
        grid=(2,),
        in_specs=in_specs,
        out_specs=(out_spec,) * 4,
        scratch_shapes=[
            vmem((SLOTS, 256), BF16),
            vmem((SLOTS, 256), BF16),
            vmem((SLOTS, HEAD_DIM), BF16),
            vmem((SLOTS, HEAD_DIM), BF16),
            vmem((HEAD_DIM, SLOTS), BF16),
            vmem((HEAD_DIM, SLOTS), BF16),
            vmem((2, SLOTS, QB), F32),
            vmem((2, SLOTS, QB), F32),
            vmem((SLOTS, SLOTS), BF16),
            vmem((SLOTS, SLOTS), BF16),
        ],
        name="attention",
    )(
        meta,
        jnp.asarray(rep, BF16),
        jnp.asarray(pick, BF16),
        jnp.asarray(base, BF16),
        pattern,
        jnp.asarray(hidden, BF16),
        arrived,
        arrived,
        arrived,
        arrived,
    )


def combine_kernel(
    slots_ref,
    key_ref,
    rms_ref,
    dk_ref,
    o_ref,
    dq_ref,
    dv_ref,
    key_home,
    o_home,
    dq_home,
    dv_home,
    held,
    placing,
    sending,
    landed,
    parts,
    key_done,
    out_sem,
    d_send,
    d_recv,
    z_send,
    z_recv,
    x_send,
    x_recv,
):
    y, z, core = place()
    d = y * 2 + core
    x = lax.axis_index("head")
    sources = (dk_ref, o_ref, dq_ref, dv_ref)
    homes = (key_home, o_home, dq_home, dv_home)
    barrier = greet(y, z, core, d, x)

    across = lax.broadcasted_iota(jnp.int32, (T_DEV, T_DEV), 1)
    down = lax.broadcasted_iota(jnp.int32, (T_DEV, T_DEV), 0)
    eye = jnp.where(down == across, 1.0, 0.0).astype(BF16)

    def build(zz):
        there = expander(slots_ref[zz], zz // 4)
        placing[zz] = contract_last(eye, there).astype(BF16)

    def d_copy(a, q, k):
        to = lax.rem(d + k, ND)
        return pltpu.make_async_remote_copy(
            src_ref=sources[a].at[to, q],
            dst_ref=held.at[a, q, d],
            send_sem=d_send.at[a, to],
            recv_sem=d_recv.at[a, q],
            device_id={"seq": along_d(to, z)},
            device_id_type=MESH,
        )

    def d_sent(a, k):
        to = lax.rem(d + k, ND)
        return pltpu.make_async_remote_copy(
            src_ref=sources[0].at[to],
            dst_ref=sources[0].at[to],
            send_sem=d_send.at[a, to],
            recv_sem=d_recv.at[a, 0],
            device_id={"seq": along_d(to, z)},
            device_id_type=MESH,
        )

    def z_copy(a, to):
        return pltpu.make_async_remote_copy(
            src_ref=sending.at[a, to],
            dst_ref=landed.at[a, :, head_columns(z)],
            send_sem=z_send.at[a, to],
            recv_sem=z_recv.at[a, z],
            device_id={"seq": along_z(y, core, to)},
            device_id_type=MESH,
        )

    def z_arrival(a, k):
        came = lax.rem(z + k, NZ)
        return pltpu.make_async_remote_copy(
            src_ref=sending.at[a, came],
            dst_ref=landed.at[a, :, head_columns(came)],
            send_sem=z_send.at[a, came],
            recv_sem=z_recv.at[a, came],
            device_id={"seq": along_z(y, core, came)},
            device_id_type=MESH,
        )

    def z_own(a):
        return pltpu.make_async_copy(
            sending.at[a, z], landed.at[a, :, head_columns(z)], z_recv.at[a, z]
        )

    x_copy, x_arrival = x_copies(x, parts, x_send, x_recv)
    pl.semaphore_wait(barrier, 17)
    for a in range(4):

        def chunk_start(o, a=a):
            q = lax.rem(z + o, 4)
            each(1, lambda k: d_copy(a, q, k).start())
            pltpu.make_async_copy(
                sources[a].at[d, q], held.at[a, q, d], d_recv.at[a, q]
            ).start()

        each(0, chunk_start, 4)

    each(0, build)

    def gather(a, carry):
        def chunk(o):
            q = lax.rem(z + o, 4)
            pltpu.make_async_copy(held.at[a, q], held.at[a, q], d_recv.at[a, q]).wait()
            rows = held[a, q].reshape(ROWS, HEAD_DIM)
            far = lax.rem(z + o + 4, NZ)
            found = jnp.dot(placing[far], rows, preferred_element_type=F32)
            sending[a, far] = found.astype(BF16)
            z_copy(a, far).start()
            close = lax.rem(z + o, NZ)
            found = jnp.dot(placing[close], rows, preferred_element_type=F32)
            sending[a, close] = found.astype(BF16)

        chunk(0)
        z_own(a).start()

        def chunk_both(o):
            chunk(o)
            z_copy(a, lax.rem(z + o, NZ)).start()

        each(1, chunk_both, 4)
        return carry

    lax.fori_loop(0, 4, gather, 0)

    def put_out(a):
        source = key_done if a == 0 else landed.at[a]
        return pltpu.make_async_copy(source, homes[a], out_sem.at[a])

    def home(a):
        z_own(a).wait()
        each(1, lambda k: z_arrival(a, k).wait_recv())

    home(0)
    key_float = key_ref[...].astype(F32)
    rms = rms_ref[:, 0:1]
    normed_float = key_float / rms
    parts[x] = lanes_summed(normed_float * landed[0].astype(F32))
    each(1, lambda k: x_copy(k).start(), NX)
    home(1)
    put_out(1).start()
    home(2)
    put_out(2).start()
    each(1, lambda k: x_arrival(k).wait_recv(), NX)
    inner = parts[0] + parts[1] + parts[2] + parts[3]
    inner = jnp.sum(inner, axis=1, keepdims=True) / (HEADS * HEAD_DIM)
    key_grad = (landed[0].astype(F32) - normed_float * inner) / rms
    key_done[...] = key_grad.astype(BF16)
    put_out(0).start()
    home(3)
    put_out(3).start()
    each(1, lambda k: x_arrival(k).wait_send(), NX)

    for a in range(4):

        def one(k, a=a):
            z_arrival(a, k).wait_send()
            d_sent(a, k).wait_send()

        each(1, one)
        put_out(a).wait()


def combine(slots, key, rms, dk, o, dq, dv):
    any_space = pl.BlockSpec(memory_space=pl.ANY)
    near = pl.BlockSpec(memory_space=pltpu.VMEM)
    dma = pltpu.SemaphoreType.DMA
    vmem = pltpu.VMEM
    home = jax.ShapeDtypeStruct((T_DEV, NZ * HEAD_DIM), BF16)
    return pl.pallas_call(
        combine_kernel,
        out_shape=(home,) * 4,
        in_specs=[near] * 3 + [any_space] * 4,
        out_specs=(any_space,) * 4,
        scratch_shapes=[
            vmem((4, NZ // 2, ND, 2, PAIR, HEAD_DIM), BF16),
            vmem((NZ, T_DEV, ROWS), BF16),
            vmem((4, NZ, T_DEV, HEAD_DIM), BF16),
            vmem((4, T_DEV, NZ * HEAD_DIM), BF16),
            vmem((NX, T_DEV, HEAD_DIM), F32),
            vmem((T_DEV, NZ * HEAD_DIM), BF16),
            dma((4,)),
            dma((4, ND)),
            dma((4, NZ // 2)),
            dma((4, NZ)),
            dma((4, NZ)),
            dma((NX,)),
            dma((NX,)),
        ],
        compiler_params=pltpu.CompilerParams(collective_id=1, has_side_effects=True),
        name="combine",
    )(slots, key, rms, dk, o, dq, dv)


def hand_over_kernel(*refs):
    ins, outs, held, in_sem, out_sem = refs[0:4], refs[4:8], refs[8], refs[9], refs[10]
    arrive = [pltpu.make_async_copy(ins[a], held.at[a], in_sem.at[a]) for a in range(4)]
    leave = [pltpu.make_async_copy(held.at[a], outs[a], out_sem.at[a]) for a in range(4)]
    for a in range(4):
        arrive[a].start()
    for a in range(4):
        arrive[a].wait()
        leave[a].start()
    for a in range(4):
        leave[a].wait()


def hand_over(*arrays):
    any_space = pl.BlockSpec(memory_space=pl.ANY)
    dma = pltpu.SemaphoreType.DMA
    return pl.pallas_call(
        hand_over_kernel,
        out_shape=tuple(jax.ShapeDtypeStruct(a.shape, a.dtype) for a in arrays),
        in_specs=[any_space] * 4,
        out_specs=(any_space,) * 4,
        scratch_shapes=[pltpu.VMEM((4,) + arrays[0].shape, BF16), dma((4,)), dma((4,))],
        name="hand_over",
    )(*arrays)


def per_device(queries, key_vectors, values, cotangent, cluster, block_pattern):
    me = lax.axis_index("seq")
    d = (me // (2 * NZ)) * 2 + me % 2
    ids = cluster.reshape(1, T_DEV)
    arrived, meta, slots, rms = dispatch(ids, key_vectors, values, cotangent, queries)
    pattern = lax.dynamic_slice_in_dim(block_pattern, 2 * d, 2, 0)
    blocks = pattern.shape[1]
    pattern = jnp.where(pattern == 1, 0.0, -BIG)
    pattern = jnp.pad(pattern, ((0, 0), (0, 0), (0, 1)), constant_values=-BIG)
    pattern = jnp.pad(pattern, ((0, 0), (0, 128 - blocks), (0, 127 - blocks))).astype(BF16)
    o, dq, dk, dv = attention(meta.reshape(64, 128), pattern, arrived)
    key_grad, attended, query_grad, value_grad = combine(slots, key_vectors, rms, dk, o, dq, dv)
    return hand_over(attended, query_grad, key_grad, value_grad)


def solution(mesh):
    in_specs = (
        P("seq", "head"),
        P("seq", "head"),
        P("seq", "head"),
        P("seq", "head"),
        P("seq", None),
        P(),
    )
    out_specs = (P("seq", "head"), P("seq", "head"), P("seq", "head"), P("seq", "head"))
    return jax.shard_map(
        per_device, mesh=mesh, in_specs=in_specs, out_specs=out_specs, check_vma=False
    )
```
